32 devices in a mesh: gx: 8 (over y, x, core), gy: 4 (over z).
Axes of the slice: x: 2, y: 2, z: 4, core: 2. Of those that a mesh axis runs over, the one named last changes fastest.
Arguments:
- permeability: float32 [8192, 1024], P('gx', 'gy'), may hold values from 0.01 to 100
- basis: float32 [64, 8, 256, 256], P('gx', 'gy'), may hold values from 0 to 1, as said below
- support: int32 [64, 8, 256, 256], P('gx', 'gy'), may hold values from 0 to 1, as said below
Outputs:
- smoothed: float32 [64, 8, 256, 256], P('gx', 'gy')
The draws below stay inside these ranges and needn't reach their ends.
Inputs may be any that keep to these rules, and one draw needn't show every extreme that they name: support is 1 exactly on a rectangle of the box that contains the block's own 128 x 128 cells in its middle and reaches 32 to 64 cells past them on each side, cut to the grid. basis is positive where support is 1 and 0 elsewhere.
All inputs are finite; a program needn't handle non-finite values.
Results may differ from the reference program's by a relative error of at most 0.0003.
Values sent between devices are 32-bit elements; how exact they have to be, the bound alone decides.
A program may use at most 128 MiB of HBM per device.

```python
import math
import jax
import jax.numpy as jnp

B = 128
H = 64
ITERS = 2
NX = 8192
NY = 1024
NBX = 64
NBY = 8


def support_parts(key):
    sides = jax.random.randint(jax.random.fold_in(key, 11), (NBX, NBY, 4), H // 2, H + 1)
    offsets = jnp.arange(2 * B, dtype=jnp.int32)
    start_x = (jnp.arange(NBX, dtype=jnp.int32) * B - H)[:, None, None] + offsets[None, None, :]
    start_y = (jnp.arange(NBY, dtype=jnp.int32) * B - H)[None, :, None] + offsets[None, None, :]
    in_x = (offsets[None, None, :] >= H - sides[:, :, 0:1]) & (offsets[None, None, :] < H + B + sides[:, :, 1:2])
    in_x = in_x & (start_x >= 0) & (start_x < NX)
    in_y = (offsets[None, None, :] >= H - sides[:, :, 2:3]) & (offsets[None, None, :] < H + B + sides[:, :, 3:4])
    in_y = in_y & (start_y >= 0) & (start_y < NY)
    return (in_x[:, :, :, None] & in_y[:, :, None, :]).astype(jnp.int32)


def draw_support(key, part):
    return support_parts(key)


def draw_basis(key, part):
    inside = support_parts(key).astype(jnp.float32)
    shape = (NBX, NBY, 2 * B, 2 * B)
    values = jnp.exp(jax.random.uniform(jax.random.fold_in(key, 23), shape, jnp.float32, jnp.log(0.05), 0.0))
    return values * inside


def levels(own_key, extent, pieces, smallest, top_value):
    loudness = 1.0
    for position, shards_of in pieces:
        draws = jax.random.uniform(jax.random.fold_in(jax.random.fold_in(own_key, 6), position), (shards_of,), jnp.float32, smallest / len(pieces), top_value / len(pieces))
        loudness = loudness * jnp.repeat(jnp.exp(draws), extent[position] // shards_of).reshape((-1,) + (1,) * (len(extent) - 1 - position))
    return loudness


def setup_inputs(seed: int = 0) -> dict:
    streams_of = jax.random.split(jax.random.key(seed), 4)
    return {
        "permeability": jnp.clip(jnp.exp(math.log(100.0) - 9.2103404 * jax.random.uniform(streams_of[0], (NX, NY), jnp.float32) ** levels(streams_of[0], (NX, NY), ((0, 8), (1, 4)), -0.2, 0.2)), 0.01, 100.0),
        "basis": draw_basis(jax.random.fold_in(streams_of[3], 71), 0),
        "support": draw_support(jax.random.fold_in(streams_of[3], 71), 0),
    }


relaxation = 2.0 / 3.0


def to_boxes(extended, count_x, count_y, block):
    tiles = extended.reshape(count_x + 1, block, count_y + 1, block).transpose(0, 2, 1, 3)
    upper = jnp.concatenate([tiles[:-1, :-1], tiles[:-1, 1:]], axis=3)
    lower = jnp.concatenate([tiles[1:, :-1], tiles[1:, 1:]], axis=3)
    return jnp.concatenate([upper, lower], axis=2)


def from_boxes(boxes, block):
    count_x, count_y = boxes.shape[0], boxes.shape[1]
    none = (0, 0)
    tiles = jnp.pad(boxes[:, :, :block, :block], ((0, 1), (0, 1), none, none))
    tiles = tiles + jnp.pad(boxes[:, :, :block, block:], ((0, 1), (1, 0), none, none))
    tiles = tiles + jnp.pad(boxes[:, :, block:, :block], ((1, 0), (0, 1), none, none))
    tiles = tiles + jnp.pad(boxes[:, :, block:, block:], ((1, 0), (1, 0), none, none))
    return tiles.transpose(0, 2, 1, 3).reshape((count_x + 1) * block, (count_y + 1) * block)


def harmonic(left, right):
    summed = left + right
    inside = summed > 0
    return jnp.where(inside, 2.0 * left * right / jnp.where(inside, summed, 1.0), 0.0)


def couplings(padded):
    faces_x = harmonic(padded[:-1, 1:-1], padded[1:, 1:-1])
    faces_y = harmonic(padded[1:-1, :-1], padded[1:-1, 1:])
    east = faces_x[1:]
    west = faces_x[:-1]
    north = faces_y[:, 1:]
    south = faces_y[:, :-1]
    diagonal = east + west + north + south
    return east, west, north, south, jnp.where(diagonal > 0, diagonal, 1.0)


def smooth(basis, support, east, west, north, south, diagonal):
    none = (0, 0)
    from_east = jnp.pad(basis[:, :, 1:, :], (none, none, (0, 1), none))
    from_west = jnp.pad(basis[:, :, :-1, :], (none, none, (1, 0), none))
    from_north = jnp.pad(basis[:, :, :, 1:], (none, none, none, (0, 1)))
    from_south = jnp.pad(basis[:, :, :, :-1], (none, none, none, (1, 0)))
    coupled = east * from_east + west * from_west + north * from_north + south * from_south
    return jnp.where(support > 0, (1.0 - relaxation) * basis + relaxation * coupled / diagonal, 0.0)


def reference(permeability, basis, support):
    padded = jnp.pad(permeability, H + 1)
    weights = tuple(to_boxes(field, NBX, NBY, B) for field in couplings(padded))
    for step in range(ITERS):
        basis = smooth(basis, support, *weights)
        summed = from_boxes(basis, B)
        summed = jnp.where(summed > 0, summed, 1.0)
        basis = basis / to_boxes(summed, NBX, NBY, B)
    return basis
```

```python
import jax
import jax.numpy as jnp
from jax import lax
from jax.experimental import pallas as pl
from jax.experimental.pallas import tpu as pltpu
from jax.sharding import PartitionSpec as P

ITERS = 2
MESH = pl.DeviceIdType.MESH
relaxation = 2.0 / 3.0
PAD = 8
CH = 32


def padded_2(shard, sides, width):
    for axis, dim in sides:
        devices, length = (lax.axis_size(axis), shard.shape[dim])
        up = [(i, (i + 1) % devices) for i in range(devices - 1)]
        down = [(j, i) for i, j in up]
        last = lax.slice_in_dim(shard, length - width, length, axis=dim)
        initial = lax.slice_in_dim(shard, 0, width, axis=dim)
        before = lax.ppermute(last, axis, up)
        after = lax.ppermute(initial, axis, down)
        shard = jnp.concatenate([before, shard, after], axis=dim)
    return shard


def harmonic(left, right):
    summed = left + right
    inside = summed > 0
    return jnp.where(inside, 2.0 * left * right / jnp.where(inside, summed, 1.0), 0.0)


def scaled_couplings(padded):
    faces_x = harmonic(padded[:-1, 1:-1], padded[1:, 1:-1])
    faces_y = harmonic(padded[1:-1, :-1], padded[1:-1, 1:])
    east = faces_x[1:]
    west = faces_x[:-1]
    north = faces_y[:, 1:]
    south = faces_y[:, :-1]
    diagonal = east + west + north + south
    scale = relaxation / jnp.where(diagonal > 0, diagonal, 1.0)
    return (east * scale, west * scale, north * scale, south * scale)


def make_kernel(nx, ny, size_x, size_y, half):
    full = 2 * half
    last = nx
    strips = ny + 1

    def kernel(*refs):
        (we_h, ww_h, wn_h, ws_h, basis_h, out_h,
         a, b, d, w, s, inv, rz, rx,
         a_sem, w_sem, o_sem, zs_sem, zr_sem, xs_sem, xr_sem) = refs
        gx, gy = lax.axis_index("gx"), lax.axis_index("gy")
        has_up, has_down = gx > 0, gx < size_x - 1
        has_left, has_right = gy > 0, gy < size_y - 1
        up, down = (gx - 1, gy), (gx + 1, gy)
        left, right = (gx, gy - 1), (gx, gy + 1)
        z_sides = ((0, has_left, left), (1, has_right, right))
        x_sides = ((0, has_up, up), (1, has_down, down))

        def row1(k):
            return jnp.where(k == 0, 0, jnp.where(k == 1, nx - 1, k - 1))

        def a_copy(i):
            return pltpu.make_async_copy(basis_h.at[i], a.at[i, :, pl.ds(PAD, full), :], a_sem.at[i])

        def w_copy(n, rb):
            src = (we_h, ww_h, wn_h, ws_h)[n]
            return pltpu.make_async_copy(
                src.at[pl.ds(pl.multiple_of(rb * half, half), half), :], w.at[n, rb], w_sem.at[n, rb])

        def o_copy(i):
            return pltpu.make_async_copy(a.at[i, :, pl.ds(PAD, full), :], out_h.at[i], o_sem.at[i])

        def z_copy(it, side, target, rb):
            strip = 0 if side == 0 else strips - 1
            return pltpu.make_async_remote_copy(
                src_ref=s.at[it, rb, strip], dst_ref=rz.at[it, 1 - side, rb],
                send_sem=zs_sem.at[it, side, rb], recv_sem=zr_sem.at[it, 1 - side, rb],
                device_id=target, device_id_type=MESH)

        def z_arrival(it, side, target, rb):
            return pltpu.make_async_remote_copy(
                src_ref=s.at[it, rb, 0], dst_ref=rz.at[it, side, rb],
                send_sem=zs_sem.at[it, side, rb], recv_sem=zr_sem.at[it, side, rb],
                device_id=target, device_id_type=MESH)

        def x_copy(it, side, target):
            rb = 0 if side == 0 else last
            return pltpu.make_async_remote_copy(
                src_ref=s.at[it, rb], dst_ref=rx.at[it, 1 - side],
                send_sem=xs_sem.at[it, side], recv_sem=xr_sem.at[it, 1 - side],
                device_id=target, device_id_type=MESH)

        def x_arrival(it, side, target):
            return pltpu.make_async_remote_copy(
                src_ref=s.at[it, 0], dst_ref=rx.at[it, side],
                send_sem=xs_sem.at[it, side], recv_sem=xr_sem.at[it, side],
                device_id=target, device_id_type=MESH)

        barrier = pltpu.get_barrier_semaphore()
        for _, has, target in z_sides + x_sides:
            @pl.when(has)
            def _():
                pl.semaphore_signal(barrier, inc=1, device_id=target, device_id_type=MESH)

        @pl.loop(0, nx)
        def _(k):
            a_copy(row1(k)).start()

        @pl.loop(0, nx + 1)
        def _(rb):
            for n in range(4):
                w_copy(n, rb).start()

        edge = jnp.zeros((PAD, full), jnp.float32)
        blank = jnp.zeros((half, half), jnp.float32)

        @pl.loop(0, nx)
        def _(i):
            for j in range(ny):
                a[i, j, 0:PAD, :] = edge
                a[i, j, PAD + full:, :] = edge
                b[i + 1, j, 0:PAD, :] = edge
                b[i + 1, j, PAD + full:, :] = edge

        for buf in (b, d):
            for j in range(ny):
                for r in range(0, full, half):
                    buf[0, j, PAD + r:PAD + r + half, :] = jnp.zeros((half, full), jnp.float32)
                    buf[nx + 1, j, PAD + r:PAD + r + half, :] = jnp.zeros((half, full), jnp.float32)

        for side, has, _t in z_sides:
            @pl.when(jnp.logical_not(has))
            def _():
                @pl.loop(0, nx + 1)
                def _(rb):
                    for it in range(ITERS):
                        rz[it, side, rb] = blank

        lanes = lax.broadcasted_iota(jnp.int32, (CH, full), 1)
        not_last, not_first = lanes < full - 1, lanes > 0

        def smooth_row(i, first):
            for j in range(ny):
                for r in range(0, full, CH):
                    lo = PAD + r
                    rb = i + r // half
                    q = r % half

                    def load(shift):
                        if first:
                            return a[i, j, lo + shift:lo + shift + CH, :]
                        return b[i + 1, j, lo + shift:lo + shift + CH, :]

                    def weight(n):
                        return w[n, rb, q:q + CH, j * half:j * half + full]

                    x = load(0)
                    ahead = jnp.where(not_last, pltpu.roll(x, full - 1, 1), 0.0)
                    behind = jnp.where(not_first, pltpu.roll(x, 1, 1), 0.0)
                    new = (1.0 - relaxation) * x + weight(0) * load(1) + weight(1) * load(-1)
                    new = new + weight(2) * ahead + weight(3) * behind
                    mask = x if first else a[i, j, lo:lo + CH, :]
                    new = jnp.where(mask > 0, new, 0.0)
                    if first:
                        b[i + 1, j, lo:lo + CH, :] = new
                    else:
                        d[i + 1, j, lo:lo + CH, :] = new

        def partial(it, rb):
            src = b if it == 0 else d
            for c in range(strips):
                for r in range(0, half, CH):
                    total = None
                    for j, lane in ((c - 1, half), (c, 0)):
                        if 0 <= j < ny:
                            low = src[rb, j, PAD + half + r:PAD + half + r + CH, lane:lane + half]
                            high = src[rb + 1, j, PAD + r:PAD + r + CH, lane:lane + half]
                            term = low + high
                            total = term if total is None else total + term
                    s[it, rb, c, r:r + CH, :] = total

        def z_send(it, rb):
            for side, has, target in z_sides:
                @pl.when(has)
                def _():
                    z_copy(it, side, target, rb).start()

        def invert(it, rb):
            for side, has, target in z_sides:
                @pl.when(has)
                def _():
                    z_arrival(it, side, target, rb).wait_recv()
            for c in range(strips):
                for r in range(0, half, CH):
                    total = s[it, rb, c, r:r + CH, :]
                    if c == 0:
                        total = total + rz[it, 0, rb, r:r + CH, :]
                    if c == strips - 1:
                        total = total + rz[it, 1, rb, r:r + CH, :]
                    inv[rb, r:r + CH, c * half:(c + 1) * half] = 1.0 / jnp.where(total > 0, total, 1.0)

        def x_send(it, side):
            _, has, target = x_sides[side]

            @pl.when(has)
            def _():
                x_copy(it, side, target).start()

        def x_add(it, side):
            _, has, target = x_sides[side]
            rb = 0 if side == 0 else last

            @pl.when(has)
            def _():
                x_copy(it, side, target).wait_send()
                x_arrival(it, side, target).wait_recv()
                for c in range(strips):
                    s[it, rb, c] = s[it, rb, c] + rx[it, side, c]

        def normalise(i, src, dst):
            for j in range(ny):
                for r in range(0, full, CH):
                    rb = i + r // half
                    q = r % half
                    lo = PAD + r
                    value = src[i + 1, j, lo:lo + CH, :] * inv[rb, q:q + CH, j * half:j * half + full]
                    if dst is None:
                        src[i + 1, j, lo:lo + CH, :] = value
                    else:
                        dst[i, j, lo:lo + CH, :] = value

        def w_wait(rb):
            for n in range(4):
                w_copy(n, rb).wait()

        peers = sum(jnp.where(has, 1, 0) for _, has, _t in z_sides + x_sides)
        pl.semaphore_wait(barrier, peers)

        @pl.loop(0, nx)
        def _(k):
            i = row1(k)
            a_copy(i).wait()

            @pl.when(k == 0)
            def _():
                w_wait(0)
                w_wait(1)

            @pl.when(k == 1)
            def _():
                w_wait(nx - 1)
                w_wait(nx)

            @pl.when((k >= 2) & (k < nx - 1))
            def _():
                w_wait(i + 1)

            smooth_row(i, True)

            @pl.when(k == 0)
            def _():
                partial(0, 0)
                x_send(0, 0)

            @pl.when(k == 1)
            def _():
                partial(0, last)
                x_send(0, 1)

            @pl.when(k >= 2)
            def _():
                partial(0, i)
                z_send(0, i)

            @pl.when(k == nx - 1)
            def _():
                partial(0, nx - 1)
                z_send(0, nx - 1)

        x_add(0, 0)
        z_send(0, 0)
        x_add(0, 1)
        z_send(0, last)

        invert(0, 1)

        @pl.loop(0, nx)
        def _(k):
            i = jnp.where(k < nx - 2, k + 1, jnp.where(k == nx - 2, 0, nx - 1))
            invert(0, jnp.where(k < nx - 2, k + 2, jnp.where(k == nx - 2, 0, nx)))
            normalise(i, b, None)
            smooth_row(i, False)

            @pl.when((k >= 1) & (k < nx - 2))
            def _():
                partial(1, i)
                z_send(1, i)

            @pl.when(k >= nx - 2)
            def _():
                rb = jnp.where(k == nx - 2, 1, nx - 1)
                partial(1, rb)
                z_send(1, rb)
                partial(1, jnp.where(k == nx - 2, 0, nx))

            @pl.when(k == nx - 2)
            def _():
                x_send(1, 0)

            @pl.when(k == nx - 1)
            def _():
                x_send(1, 1)

        x_add(1, 0)
        z_send(1, 0)
        x_add(1, 1)
        z_send(1, last)

        invert(1, 2)

        @pl.loop(0, nx)
        def _(k):
            n = nx - 4
            i = jnp.where(k < n, k + 2, jnp.where(k == n, 1, jnp.where(
                k == n + 1, nx - 2, jnp.where(k == n + 2, 0, nx - 1))))
            rb = jnp.where(k < n, k + 3, jnp.where(k == n, 1, jnp.where(
                k == n + 1, nx - 1, jnp.where(k == n + 2, 0, nx))))
            invert(1, rb)
            normalise(i, d, a)
            o_copy(i).start()

        @pl.loop(0, nx)
        def _(i):
            o_copy(i).wait()

        for side, has, target in z_sides:
            @pl.when(has)
            def _():
                @pl.loop(0, nx + 1)
                def _(rb):
                    for it in range(ITERS):
                        z_copy(it, side, target, rb).wait_send()

    return kernel


def local(permeability, basis, support):
    nx, ny, full, _ = basis.shape
    half = full // 2
    size_x, size_y = lax.axis_size("gx"), lax.axis_size("gy")
    padded = padded_2(permeability, (("gx", 0), ("gy", 1)), half // 2 + 1)
    weights = scaled_couplings(padded)
    f32 = jnp.float32
    strips = ny + 1
    scratch = [
        pltpu.VMEM((nx, ny, full + 2 * PAD, full), f32),
        pltpu.VMEM((nx + 2, ny, full + 2 * PAD, full), f32),
        pltpu.VMEM((nx + 2, ny, full + 2 * PAD, full), f32),
        pltpu.VMEM((4, nx + 1, half, strips * half), f32),
        pltpu.VMEM((ITERS, nx + 1, strips, half, half), f32),
        pltpu.VMEM((nx + 1, half, strips * half), f32),
        pltpu.VMEM((ITERS, 2, nx + 1, half, half), f32),
        pltpu.VMEM((ITERS, 2, strips, half, half), f32),
        pltpu.SemaphoreType.DMA((nx,)),
        pltpu.SemaphoreType.DMA((4, nx + 1)),
        pltpu.SemaphoreType.DMA((nx,)),
        pltpu.SemaphoreType.DMA((ITERS, 2, nx + 1)),
        pltpu.SemaphoreType.DMA((ITERS, 2, nx + 1)),
        pltpu.SemaphoreType.DMA((ITERS, 2)),
        pltpu.SemaphoreType.DMA((ITERS, 2)),
    ]
    return pl.pallas_call(
        make_kernel(nx, ny, size_x, size_y, half),
        out_shape=jax.ShapeDtypeStruct(basis.shape, f32),
        in_specs=[pl.BlockSpec(memory_space=pl.ANY)] * 5,
        out_specs=pl.BlockSpec(memory_space=pl.ANY),
        scratch_shapes=scratch,
        compiler_params=pltpu.CompilerParams(
            collective_id=0, has_side_effects=True, vmem_limit_bytes=48 * 1024 * 1024),
        name="smoothing",
    )(*weights, basis)


def solution(mesh):
    placed = (P("gx", "gy"), P("gx", "gy", None, None), P("gx", "gy", None, None))
    return jax.shard_map(
        local, mesh=mesh, in_specs=placed, out_specs=P("gx", "gy", None, None), check_vma=False
    )
```

```python
import jax
import jax.numpy as jnp
from jax import lax
from jax.experimental import pallas as pl
from jax.experimental.pallas import tpu as pltpu
from jax.sharding import PartitionSpec as P

ITERS = 2
MESH = pl.DeviceIdType.MESH
relaxation = 2.0 / 3.0
PAD = 8
CH = 32


def harmonic(left, right):
    return 2.0 * left * right / jnp.maximum(left + right, 1e-30)


def pick(k, table):
    value = jnp.int32(table[-1])
    for n in range(len(table) - 2, -1, -1):
        value = jnp.where(k == n, table[n], value)
    return value


def completed(rows, count):
    done, out = set(), []
    for i in rows:
        done.add(i)
        new = [rb for rb in (i, i + 1) if 0 < rb < count and rb - 1 in done and rb in done]
        assert len(new) <= 1
        out.append(new[0] if new else -1)
    return out


def needed(rows):
    seen, out = set(), []
    for i in rows:
        new = [rb for rb in (i, i + 1) if rb not in seen]
        seen.update(new)
        out.append(new)
    return out


def make_kernel(nx, ny, size_x, size_y, half):
    full = 2 * half
    last = nx
    strips = ny + 1

    def kernel(*refs):
        (perm_h, basis_h, out_h,
         a, b, d, w, s, inv, rz, rx, px, pe, pk, pr, hk, hr,
         a_sem, p_sem, o_sem, zs_sem, zr_sem, xs_sem, xr_sem,
         ps_sem, pr_sem, hs_sem, hr_sem, rs_sem, rr_sem) = refs
        gx, gy = lax.axis_index("gx"), lax.axis_index("gy")
        has_up, has_down = gx > 0, gx < size_x - 1
        has_left, has_right = gy > 0, gy < size_y - 1
        up, down = (gx - 1, gy), (gx + 1, gy)
        left, right = (gx, gy - 1), (gx, gy + 1)
        z_sides = ((0, has_left, left), (1, has_right, right))
        x_sides = ((0, has_up, up), (1, has_down, down))

        rows_1 = list(range(2, nx - 2)) + [1, nx - 2, 0, nx - 1]
        rows_2 = list(range(3, nx - 3)) + [2, nx - 3, 1, nx - 2, 0, nx - 1]
        need_1, need_2 = needed(rows_1), needed(rows_2)
        ready_1, ready_2 = completed(rows_1, nx), completed(rows_2, nx)
        halo = half // 2 + PAD
        height = px.shape[0]
        length = height - 2 * halo
        hw = half // 2

        def a_copy(i):
            return pltpu.make_async_copy(basis_h.at[i], a.at[i, :, pl.ds(PAD, full), :], a_sem.at[i])

        def row_copy(side, target):
            src = 0 if side == 0 else length - halo
            dst = height - halo if side == 0 else 0
            return pltpu.make_async_remote_copy(
                src_ref=perm_h.at[pl.ds(src, halo), :], dst_ref=px.at[pl.ds(dst, halo), :],
                send_sem=rs_sem.at[side], recv_sem=rr_sem.at[1 - side],
                device_id=target, device_id_type=MESH)

        def row_arrival(side, target):
            dst = 0 if side == 0 else height - halo
            return pltpu.make_async_remote_copy(
                src_ref=perm_h.at[pl.ds(0, halo), :], dst_ref=px.at[pl.ds(dst, halo), :],
                send_sem=rs_sem.at[side], recv_sem=rr_sem.at[side],
                device_id=target, device_id_type=MESH)

        def pk_copy(side, target, rb):
            return pltpu.make_async_remote_copy(
                src_ref=pk.at[side, rb], dst_ref=pr.at[1 - side, rb],
                send_sem=ps_sem.at[side, rb], recv_sem=pr_sem.at[1 - side, rb],
                device_id=target, device_id_type=MESH)

        def pk_arrival(side, target, rb):
            return pltpu.make_async_remote_copy(
                src_ref=pk.at[side, rb], dst_ref=pr.at[side, rb],
                send_sem=ps_sem.at[side, rb], recv_sem=pr_sem.at[side, rb],
                device_id=target, device_id_type=MESH)

        def hk_copy(side, target):
            return pltpu.make_async_remote_copy(
                src_ref=hk, dst_ref=hr.at[1 - side],
                send_sem=hs_sem.at[side], recv_sem=hr_sem.at[1 - side],
                device_id=target, device_id_type=MESH)

        def hk_arrival(side, target):
            return pltpu.make_async_remote_copy(
                src_ref=hk, dst_ref=hr.at[side],
                send_sem=hs_sem.at[side], recv_sem=hr_sem.at[side],
                device_id=target, device_id_type=MESH)

        def o_copy(i):
            return pltpu.make_async_copy(a.at[i, :, pl.ds(PAD, full), :], out_h.at[i], o_sem.at[i])

        def z_copy(it, side, target, rb):
            strip = 0 if side == 0 else strips - 1
            return pltpu.make_async_remote_copy(
                src_ref=s.at[it, rb, strip], dst_ref=rz.at[it, 1 - side, rb],
                send_sem=zs_sem.at[it, side, rb], recv_sem=zr_sem.at[it, 1 - side, rb],
                device_id=target, device_id_type=MESH)

        def z_arrival(it, side, target, rb):
            return pltpu.make_async_remote_copy(
                src_ref=s.at[it, rb, 0], dst_ref=rz.at[it, side, rb],
                send_sem=zs_sem.at[it, side, rb], recv_sem=zr_sem.at[it, side, rb],
                device_id=target, device_id_type=MESH)

        def x_copy(it, side, target):
            rb = 0 if side == 0 else last
            return pltpu.make_async_remote_copy(
                src_ref=s.at[it, rb], dst_ref=rx.at[it, 1 - side],
                send_sem=xs_sem.at[it, side], recv_sem=xr_sem.at[it, 1 - side],
                device_id=target, device_id_type=MESH)

        def x_arrival(it, side, target):
            return pltpu.make_async_remote_copy(
                src_ref=s.at[it, 0], dst_ref=rx.at[it, side],
                send_sem=xs_sem.at[it, side], recv_sem=xr_sem.at[it, side],
                device_id=target, device_id_type=MESH)

        barrier = pltpu.get_barrier_semaphore()
        for _, has, target in z_sides + x_sides:
            @pl.when(has)
            def _():
                pl.semaphore_signal(barrier, inc=1, device_id=target, device_id_type=MESH)

        own = pltpu.make_async_copy(perm_h, px.at[pl.ds(halo, length), :], p_sem)
        own.start()

        @pl.loop(0, nx)
        def _(k):
            a_copy(pick(k, rows_1)).start()

        edge = jnp.zeros((PAD, full), jnp.float32)
        blank = jnp.zeros((half, half), jnp.float32)

        @pl.loop(0, nx)
        def _(i):
            for j in range(ny):
                a[i, j, 0:PAD, :] = edge
                a[i, j, PAD + full:, :] = edge
                b[i + 1, j, 0:PAD, :] = edge
                b[i + 1, j, PAD + full:, :] = edge

        for buf in (b, d):
            for j in range(ny):
                for r in range(0, full, half):
                    buf[0, j, PAD + r:PAD + r + half, :] = jnp.zeros((half, full), jnp.float32)
                    buf[nx + 1, j, PAD + r:PAD + r + half, :] = jnp.zeros((half, full), jnp.float32)

        for side, has, _t in z_sides:
            @pl.when(jnp.logical_not(has))
            def _():
                @pl.loop(0, nx + 1)
                def _(rb):
                    for it in range(ITERS):
                        rz[it, side, rb] = blank
                    pr[side, rb] = jnp.zeros((hw + PAD, half), jnp.float32)
                hr[side] = jnp.zeros((2, PAD, half), jnp.float32)

        for side, has, _t in x_sides:
            @pl.when(jnp.logical_not(has))
            def _():
                lo = 0 if side == 0 else height - halo
                px[lo:lo + halo, :] = jnp.zeros((halo, full), jnp.float32)

        lanes = lax.broadcasted_iota(jnp.int32, (CH, full), 1)
        not_last, not_first = lanes < full - 1, lanes > 0

        def smooth_row(i, first):
            for j in range(ny):
                for r in range(0, full, CH):
                    lo = PAD + r
                    rb = i + r // half
                    q = r % half

                    def load(shift):
                        if first:
                            return a[i, j, lo + shift:lo + shift + CH, :]
                        return b[i + 1, j, lo + shift:lo + shift + CH, :]

                    def weight(n):
                        return w[n, rb, q:q + CH, j * half:j * half + full]

                    x = load(0)
                    ahead = jnp.where(not_last, pltpu.roll(x, full - 1, 1), 0.0)
                    behind = jnp.where(not_first, pltpu.roll(x, 1, 1), 0.0)
                    new = (1.0 - relaxation) * x + weight(0) * load(1) + weight(1) * load(-1)
                    new = new + weight(2) * ahead + weight(3) * behind
                    mask = x if first else a[i, j, lo:lo + CH, :]
                    new = jnp.where(mask > 0, new, 0.0)
                    if first:
                        b[i + 1, j, lo:lo + CH, :] = new
                    else:
                        d[i + 1, j, lo:lo + CH, :] = new

        def partial(it, rb):
            src = b if it == 0 else d
            for c in range(strips):
                for r in range(0, half, CH):
                    total = None
                    for j, lane in ((c - 1, half), (c, 0)):
                        if 0 <= j < ny:
                            low = src[rb, j, PAD + half + r:PAD + half + r + CH, lane:lane + half]
                            high = src[rb + 1, j, PAD + r:PAD + r + CH, lane:lane + half]
                            term = low + high
                            total = term if total is None else total + term
                    s[it, rb, c, r:r + CH, :] = total

        def z_send(it, rb):
            for side, has, target in z_sides:
                @pl.when(has)
                def _():
                    z_copy(it, side, target, rb).start()

        def invert(it, rb):
            for side, has, target in z_sides:
                @pl.when(has)
                def _():
                    z_arrival(it, side, target, rb).wait_recv()
            for c in range(strips):
                for r in range(0, half, CH):
                    total = s[it, rb, c, r:r + CH, :]
                    if c == 0:
                        total = total + rz[it, 0, rb, r:r + CH, :]
                    if c == strips - 1:
                        total = total + rz[it, 1, rb, r:r + CH, :]
                    inv[rb, r:r + CH, c * half:(c + 1) * half] = 1.0 / jnp.where(total > 0, total, 1.0)

        def x_send(it, side):
            _, has, target = x_sides[side]

            @pl.when(has)
            def _():
                x_copy(it, side, target).start()

        def x_add(it, side):
            _, has, target = x_sides[side]
            rb = 0 if side == 0 else last

            @pl.when(has)
            def _():
                x_copy(it, side, target).wait_send()
                x_arrival(it, side, target).wait_recv()
                for c in range(strips):
                    s[it, rb, c] = s[it, rb, c] + rx[it, side, c]

        def normalise(i, src, dst):
            for j in range(ny):
                for r in range(0, full, CH):
                    rb = i + r // half
                    q = r % half
                    lo = PAD + r
                    value = src[i + 1, j, lo:lo + CH, :] * inv[rb, q:q + CH, j * half:j * half + full]
                    if dst is None:
                        src[i + 1, j, lo:lo + CH, :] = value
                    else:
                        dst[i, j, lo:lo + CH, :] = value

        lane = lax.broadcasted_iota(jnp.int32, (hw, half), 1)
        low_half = lane < hw
        lane8 = lax.broadcasted_iota(jnp.int32, (PAD, half), 1)

        def shifted_rows(lo, count):
            return pltpu.roll(px[pl.ds(lo, count), :], hw, 1)

        def pack(rb):
            lo = pl.multiple_of(rb * half + PAD, PAD)
            first = shifted_rows(lo, hw)
            second = shifted_rows(lo + hw, hw)
            m0, m1 = first[:, :half], second[:, :half]
            pk[1, rb, 0:hw, :] = jnp.where(low_half, m0, pltpu.roll(m1, hw, 1))
            pk[0, rb, 0:hw, :] = jnp.where(low_half, pltpu.roll(m0, hw, 1), m1)
            to_left = jnp.zeros((PAD, half), jnp.float32)
            to_right = to_left
            for k in range(half // PAD):
                part = first if k * PAD < hw else second
                q = k * PAD % hw
                e = part[q:q + PAD, half:]
                here = lane8 == k
                to_left = jnp.where(here, pltpu.roll(e, k, 1) if k else e, to_left)
                to_right = jnp.where(here, pltpu.roll(e, k + 1, 1), to_right)
            pk[0, rb, hw:hw + PAD, :] = to_left
            pk[1, rb, hw:hw + PAD, :] = to_right
            for side, has, target in z_sides:
                @pl.when(has)
                def _():
                    pk_copy(side, target, rb).start()

        def pack_ends():
            for n, lo in ((0, 0), (1, height - PAD)):
                hk[n] = shifted_rows(lo, PAD)[:, :half]
            for side, has, target in z_sides:
                @pl.when(has)
                def _():
                    hk_copy(side, target).start()

        def unpack(rb):
            for side, has, target in z_sides:
                @pl.when(has)
                def _():
                    pk_arrival(side, target, rb).wait_recv()
            lo = pl.multiple_of(rb * half + PAD, PAD)
            from_left, from_right = pr[0, rb, 0:hw, :], pr[1, rb, 0:hw, :]
            for n in range(2):
                start = lo + n * hw
                rolled = shifted_rows(start, hw)
                m = rolled[:, :half]
                fl = pltpu.roll(from_left, hw, 1) if n else from_left
                fr = from_right if n else pltpu.roll(from_right, hw, 1)
                pe[pl.ds(start, hw), half:2 * half] = jnp.where(low_half, fl, m)
                pe[pl.ds(start, hw), 2 * half:3 * half] = rolled[:, half:]
                pe[pl.ds(start, hw), 3 * half:4 * half] = jnp.where(low_half, m, fr)
            cl, cr = pr[0, rb, hw:hw + PAD, :], pr[1, rb, hw:hw + PAD, :]
            for k in range(half // PAD):
                pe[pl.ds(lo + k * PAD, PAD), 0:half] = pltpu.roll(cl, half - 1 - k, 1)
                pe[pl.ds(lo + k * PAD, PAD), 4 * half:5 * half] = pltpu.roll(cr, half - k, 1) if k else cr

        def unpack_ends():
            for side, has, target in z_sides:
                @pl.when(has)
                def _():
                    hk_arrival(side, target).wait_recv()
            low8 = lane8 < hw
            for n, lo in ((0, 0), (1, height - PAD)):
                rolled = shifted_rows(lo, PAD)
                m = rolled[:, :half]
                pe[lo:lo + PAD, half:2 * half] = jnp.where(low8, hr[0, n], m)
                pe[lo:lo + PAD, 2 * half:3 * half] = rolled[:, half:]
                pe[lo:lo + PAD, 3 * half:4 * half] = jnp.where(low8, m, hr[1, n])

        wide = (strips + 2) * half
        step = 2 * PAD

        def weigh(rb):
            @pl.loop(0, half // step)
            def _(c):
                q = pl.multiple_of(c * step, step)
                lo = pl.multiple_of(rb * half + PAD + q, PAD)
                block = pe[pl.ds(lo - PAD, step + 2 * PAD), half:wide - half]
                line = pe[pl.ds(lo, step), :]
                mid = block[PAD:PAD + step]
                fx = harmonic(block[PAD - 1:PAD + step], block[PAD:PAD + step + 1])
                fy = harmonic(line, pltpu.roll(line, wide - 1, 1))
                east, west = fx[1:], fx[:-1]
                north = fy[:, half:wide - half]
                south = pltpu.roll(fy, 1, 1)[:, half:wide - half]
                diagonal = east + west + north + south
                scale = relaxation / jnp.where(diagonal > 0, diagonal, 1.0)
                for n, face in enumerate((east, west, north, south)):
                    w[n, rb, pl.ds(q, step), :] = face * scale

        peers = sum(jnp.where(has, 1, 0) for _, has, _t in z_sides + x_sides)
        pl.semaphore_wait(barrier, peers)

        for side, has, target in x_sides:
            @pl.when(has)
            def _():
                row_copy(side, target).start()
        own.wait()

        @pl.loop(1, nx)
        def _(rb):
            pack(rb)

        for side, has, target in x_sides:
            @pl.when(has)
            def _():
                row_arrival(side, target).wait_recv()

        @pl.loop(0, 2)
        def _(n):
            pack(n * nx)

        pack_ends()

        @pl.loop(1, 4)
        def _(rb):
            unpack(rb)

        weigh(need_1[0][0])

        def finish(it, k, i, ready):
            rb = pick(k, ready)

            @pl.when(rb >= 0)
            def _():
                partial(it, rb)
                z_send(it, rb)

            @pl.when(k >= nx - 2)
            def _():
                partial(it, jnp.where(i == 0, 0, nx))

            @pl.when(k == nx - 2)
            def _():
                x_send(it, 0)

            @pl.when(k == nx - 1)
            def _():
                x_send(it, 1)

        next_pe = [4 + k for k in range(nx - 4)] + [0, nx, -1, -1]

        @pl.loop(0, nx)
        def _(k):
            i = pick(k, rows_1)
            a_copy(i).wait()
            nxt = pick(k, next_pe)

            @pl.when(nxt >= 0)
            def _():
                unpack(nxt)

            @pl.when(k == nx - 2)
            def _():
                unpack_ends()

            weigh(pick(k, [n[-1] for n in need_1]))
            smooth_row(i, True)
            finish(0, k, i, ready_1)

        x_add(0, 0)
        z_send(0, 0)
        x_add(0, 1)
        z_send(0, last)

        invert(0, need_2[0][0])

        @pl.loop(0, nx)
        def _(k):
            i = pick(k, rows_2)
            invert(0, pick(k, [n[-1] for n in need_2]))
            normalise(i, b, None)
            smooth_row(i, False)
            finish(1, k, i, ready_2)

        x_add(1, 0)
        z_send(1, 0)
        x_add(1, 1)
        z_send(1, last)

        invert(1, need_2[0][-1])

        @pl.loop(0, nx)
        def _(k):
            i = pick(k, rows_2)
            invert(1, pick(k, [need_2[0][0]] + [n[-1] for n in need_2[1:]]))
            normalise(i, d, a)
            o_copy(i).start()

        @pl.loop(0, nx)
        def _(i):
            o_copy(i).wait()

        for side, has, target in z_sides:
            @pl.when(has)
            def _():
                @pl.loop(0, nx + 1)
                def _(rb):
                    for it in range(ITERS):
                        z_copy(it, side, target, rb).wait_send()
                    pk_copy(side, target, rb).wait_send()
                hk_copy(side, target).wait_send()

        for side, has, target in x_sides:
            @pl.when(has)
            def _():
                row_copy(side, target).wait_send()

    return kernel


def local(permeability, basis, support):
    nx, ny, full, _ = basis.shape
    half = full // 2
    size_x, size_y = lax.axis_size("gx"), lax.axis_size("gy")
    height = permeability.shape[0] + half + 2 * PAD
    f32 = jnp.float32
    strips = ny + 1
    scratch = [
        pltpu.VMEM((nx, ny, full + 2 * PAD, full), f32),
        pltpu.VMEM((nx + 2, ny, full + 2 * PAD, full), f32),
        pltpu.VMEM((nx + 2, ny, full + 2 * PAD, full), f32),
        pltpu.VMEM((4, nx + 1, half, strips * half), f32),
        pltpu.VMEM((ITERS, nx + 1, strips, half, half), f32),
        pltpu.VMEM((nx + 1, half, strips * half), f32),
        pltpu.VMEM((ITERS, 2, nx + 1, half, half), f32),
        pltpu.VMEM((ITERS, 2, strips, half, half), f32),
        pltpu.VMEM((height, full), f32),
        pltpu.VMEM((height, (strips + 2) * half), f32),
        pltpu.VMEM((2, nx + 1, half // 2 + PAD, half), f32),
        pltpu.VMEM((2, nx + 1, half // 2 + PAD, half), f32),
        pltpu.VMEM((2, PAD, half), f32),
        pltpu.VMEM((2, 2, PAD, half), f32),
        pltpu.SemaphoreType.DMA((nx,)),
        pltpu.SemaphoreType.DMA,
        pltpu.SemaphoreType.DMA((nx,)),
        pltpu.SemaphoreType.DMA((ITERS, 2, nx + 1)),
        pltpu.SemaphoreType.DMA((ITERS, 2, nx + 1)),
        pltpu.SemaphoreType.DMA((ITERS, 2)),
        pltpu.SemaphoreType.DMA((ITERS, 2)),
        pltpu.SemaphoreType.DMA((2, nx + 1)),
        pltpu.SemaphoreType.DMA((2, nx + 1)),
        pltpu.SemaphoreType.DMA((2,)),
        pltpu.SemaphoreType.DMA((2,)),
        pltpu.SemaphoreType.DMA((2,)),
        pltpu.SemaphoreType.DMA((2,)),
    ]
    return pl.pallas_call(
        make_kernel(nx, ny, size_x, size_y, half),
        out_shape=jax.ShapeDtypeStruct(basis.shape, f32),
        in_specs=[pl.BlockSpec(memory_space=pl.ANY)] * 2,
        out_specs=pl.BlockSpec(memory_space=pl.ANY),
        scratch_shapes=scratch,
        compiler_params=pltpu.CompilerParams(
            collective_id=0, has_side_effects=True, vmem_limit_bytes=48 * 1024 * 1024),
        name="smoothing",
    )(permeability, basis)


def solution(mesh):
    placed = (P("gx", "gy"), P("gx", "gy", None, None), P("gx", "gy", None, None))
    return jax.shard_map(
        local, mesh=mesh, in_specs=placed, out_specs=P("gx", "gy", None, None), check_vma=False
    )
```

```python
import jax
import jax.numpy as jnp
from jax import lax
from jax.experimental import pallas as pl
from jax.experimental.pallas import tpu as pltpu
from jax.sharding import PartitionSpec as P

ITERS = 2
MESH = pl.DeviceIdType.MESH
relaxation = 2.0 / 3.0
PAD = 8
CH = 32


def pick(k, table):
    value = jnp.int32(table[-1])
    for n in range(len(table) - 2, -1, -1):
        value = jnp.where(k == n, table[n], value)
    return value


def completed(rows, count):
    done, out = set(), []
    for i in rows:
        done.add(i)
        new = [rb for rb in (i, i + 1) if 0 < rb < count and rb - 1 in done and rb in done]
        assert len(new) <= 1
        out.append(new[0] if new else -1)
    return out


def needed(rows):
    seen, out = set(), []
    for i in rows:
        new = [rb for rb in (i, i + 1) if rb not in seen]
        seen.update(new)
        out.append(new)
    return out


def make_kernel(nx, ny, size_x, size_y, half):
    full = 2 * half
    last = nx
    strips = ny + 1

    def kernel(*refs):
        (perm_h, basis_h, out_h,
         a, b, d, w, s, inv, rz, rx, px, pe, pk, pr, hk, hr,
         a_sem, p_sem, o_sem, zs_sem, zr_sem, xs_sem, xr_sem,
         ps_sem, pr_sem, hs_sem, hr_sem, rs_sem, rr_sem) = refs
        gx, gy = lax.axis_index("gx"), lax.axis_index("gy")
        has_up, has_down = gx > 0, gx < size_x - 1
        has_left, has_right = gy > 0, gy < size_y - 1
        up, down = (gx - 1, gy), (gx + 1, gy)
        left, right = (gx, gy - 1), (gx, gy + 1)
        z_sides = ((0, has_left, left), (1, has_right, right))
        x_sides = ((0, has_up, up), (1, has_down, down))

        rows_1 = list(range(2, nx - 2)) + [1, nx - 2, 0, nx - 1]
        rows_2 = list(range(3, nx - 3)) + [2, nx - 3, 1, nx - 2, 0, nx - 1]
        need_1, need_2 = needed(rows_1), needed(rows_2)
        ready_1, ready_2 = completed(rows_1, nx), completed(rows_2, nx)
        halo = half // 2 + PAD
        height = px.shape[0]
        length = height - 2 * halo
        hw = half // 2

        def a_copy(i):
            return pltpu.make_async_copy(basis_h.at[i], a.at[i, :, pl.ds(PAD, full), :], a_sem.at[i])

        def row_copy(side, target):
            src = 0 if side == 0 else length - halo
            dst = height - halo if side == 0 else 0
            return pltpu.make_async_remote_copy(
                src_ref=perm_h.at[pl.ds(src, halo), :], dst_ref=px.at[pl.ds(dst, halo), :],
                send_sem=rs_sem.at[side], recv_sem=rr_sem.at[1 - side],
                device_id=target, device_id_type=MESH)

        def row_arrival(side, target):
            dst = 0 if side == 0 else height - halo
            return pltpu.make_async_remote_copy(
                src_ref=perm_h.at[pl.ds(0, halo), :], dst_ref=px.at[pl.ds(dst, halo), :],
                send_sem=rs_sem.at[side], recv_sem=rr_sem.at[side],
                device_id=target, device_id_type=MESH)

        def pk_copy(side, target, rb):
            return pltpu.make_async_remote_copy(
                src_ref=pk.at[side, rb], dst_ref=pr.at[1 - side, rb],
                send_sem=ps_sem.at[side, rb], recv_sem=pr_sem.at[1 - side, rb],
                device_id=target, device_id_type=MESH)

        def pk_arrival(side, target, rb):
            return pltpu.make_async_remote_copy(
                src_ref=pk.at[side, rb], dst_ref=pr.at[side, rb],
                send_sem=ps_sem.at[side, rb], recv_sem=pr_sem.at[side, rb],
                device_id=target, device_id_type=MESH)

        def hk_copy(side, target):
            return pltpu.make_async_remote_copy(
                src_ref=hk, dst_ref=hr.at[1 - side],
                send_sem=hs_sem.at[side], recv_sem=hr_sem.at[1 - side],
                device_id=target, device_id_type=MESH)

        def hk_arrival(side, target):
            return pltpu.make_async_remote_copy(
                src_ref=hk, dst_ref=hr.at[side],
                send_sem=hs_sem.at[side], recv_sem=hr_sem.at[side],
                device_id=target, device_id_type=MESH)

        def o_copy(i):
            return pltpu.make_async_copy(a.at[i, :, pl.ds(PAD, full), :], out_h.at[i], o_sem.at[i])

        def z_copy(it, side, target, rb):
            strip = 0 if side == 0 else strips - 1
            return pltpu.make_async_remote_copy(
                src_ref=s.at[it, rb, strip], dst_ref=rz.at[it, 1 - side, rb],
                send_sem=zs_sem.at[it, side, rb], recv_sem=zr_sem.at[it, 1 - side, rb],
                device_id=target, device_id_type=MESH)

        def z_arrival(it, side, target, rb):
            return pltpu.make_async_remote_copy(
                src_ref=s.at[it, rb, 0], dst_ref=rz.at[it, side, rb],
                send_sem=zs_sem.at[it, side, rb], recv_sem=zr_sem.at[it, side, rb],
                device_id=target, device_id_type=MESH)

        def x_copy(it, side, target):
            rb = 0 if side == 0 else last
            return pltpu.make_async_remote_copy(
                src_ref=s.at[it, rb], dst_ref=rx.at[it, 1 - side],
                send_sem=xs_sem.at[it, side], recv_sem=xr_sem.at[it, 1 - side],
                device_id=target, device_id_type=MESH)

        def x_arrival(it, side, target):
            return pltpu.make_async_remote_copy(
                src_ref=s.at[it, 0], dst_ref=rx.at[it, side],
                send_sem=xs_sem.at[it, side], recv_sem=xr_sem.at[it, side],
                device_id=target, device_id_type=MESH)

        barrier = pltpu.get_barrier_semaphore()
        for _, has, target in z_sides + x_sides:
            @pl.when(has)
            def _():
                pl.semaphore_signal(barrier, inc=1, device_id=target, device_id_type=MESH)

        own = pltpu.make_async_copy(perm_h, px.at[pl.ds(halo, length), :], p_sem)
        own.start()

        @pl.loop(0, nx)
        def _(k):
            a_copy(pick(k, rows_1)).start()

        edge = jnp.zeros((PAD, full), jnp.float32)
        blank = jnp.zeros((half, half), jnp.float32)

        @pl.loop(0, nx)
        def _(i):
            for j in range(ny):
                a[i, j, 0:PAD, :] = edge
                a[i, j, PAD + full:, :] = edge
                b[i + 1, j, 0:PAD, :] = edge
                b[i + 1, j, PAD + full:, :] = edge

        for buf in (b, d):
            for j in range(ny):
                for r in range(0, full, half):
                    buf[0, j, PAD + r:PAD + r + half, :] = jnp.zeros((half, full), jnp.float32)
                    buf[nx + 1, j, PAD + r:PAD + r + half, :] = jnp.zeros((half, full), jnp.float32)

        for side, has, _t in z_sides:
            @pl.when(jnp.logical_not(has))
            def _():
                @pl.loop(0, nx + 1)
                def _(rb):
                    for it in range(ITERS):
                        rz[it, side, rb] = blank
                    pr[side, rb] = jnp.zeros((hw + PAD, half), jnp.float32)
                hr[side] = jnp.zeros((2, PAD, half), jnp.float32)

        for side, has, _t in x_sides:
            @pl.when(jnp.logical_not(has))
            def _():
                lo = 0 if side == 0 else height - halo
                px[lo:lo + halo, :] = jnp.zeros((halo, full), jnp.float32)

        lanes = lax.broadcasted_iota(jnp.int32, (CH, full), 1)
        not_last, not_first = lanes < full - 1, lanes > 0

        def smooth_row(i, first):
            for j in range(ny):
                for r in range(0, full, CH):
                    lo = PAD + r
                    rb = i + r // half
                    q = r % half

                    def load(shift):
                        if first:
                            return a[i, j, lo + shift:lo + shift + CH, :]
                        return b[i + 1, j, lo + shift:lo + shift + CH, :]

                    def weight(n):
                        return w[n, rb, q:q + CH, j * half:j * half + full]

                    x = load(0)
                    ahead = jnp.where(not_last, pltpu.roll(x, full - 1, 1), 0.0)
                    behind = jnp.where(not_first, pltpu.roll(x, 1, 1), 0.0)
                    new = (1.0 - relaxation) * x + weight(0) * load(1) + weight(1) * load(-1)
                    new = new + weight(2) * ahead + weight(3) * behind
                    mask = x if first else a[i, j, lo:lo + CH, :]
                    new = jnp.where(mask > 0, new, 0.0)
                    if first:
                        b[i + 1, j, lo:lo + CH, :] = new
                    else:
                        d[i + 1, j, lo:lo + CH, :] = new

        def partial(it, rb):
            src = b if it == 0 else d
            for c in range(strips):
                for r in range(0, half, CH):
                    total = None
                    for j, lane in ((c - 1, half), (c, 0)):
                        if 0 <= j < ny:
                            low = src[rb, j, PAD + half + r:PAD + half + r + CH, lane:lane + half]
                            high = src[rb + 1, j, PAD + r:PAD + r + CH, lane:lane + half]
                            term = low + high
                            total = term if total is None else total + term
                    s[it, rb, c, r:r + CH, :] = total

        def z_send(it, rb):
            for side, has, target in z_sides:
                @pl.when(has)
                def _():
                    z_copy(it, side, target, rb).start()

        def invert(it, rb):
            for side, has, target in z_sides:
                @pl.when(has)
                def _():
                    z_arrival(it, side, target, rb).wait_recv()
            for c in range(strips):
                for r in range(0, half, CH):
                    total = s[it, rb, c, r:r + CH, :]
                    if c == 0:
                        total = total + rz[it, 0, rb, r:r + CH, :]
                    if c == strips - 1:
                        total = total + rz[it, 1, rb, r:r + CH, :]
                    inv[rb, r:r + CH, c * half:(c + 1) * half] = 1.0 / jnp.where(total > 0, total, 1.0)

        def x_send(it, side):
            _, has, target = x_sides[side]

            @pl.when(has)
            def _():
                x_copy(it, side, target).start()

        def x_add(it, side):
            _, has, target = x_sides[side]
            rb = 0 if side == 0 else last

            @pl.when(has)
            def _():
                x_copy(it, side, target).wait_send()
                x_arrival(it, side, target).wait_recv()
                for c in range(strips):
                    s[it, rb, c] = s[it, rb, c] + rx[it, side, c]

        def normalise(i, src, dst):
            for j in range(ny):
                for r in range(0, full, CH):
                    rb = i + r // half
                    q = r % half
                    lo = PAD + r
                    value = src[i + 1, j, lo:lo + CH, :] * inv[rb, q:q + CH, j * half:j * half + full]
                    if dst is None:
                        src[i + 1, j, lo:lo + CH, :] = value
                    else:
                        dst[i, j, lo:lo + CH, :] = value

        lane = lax.broadcasted_iota(jnp.int32, (hw, half), 1)
        low_half = lane < hw
        lane8 = lax.broadcasted_iota(jnp.int32, (PAD, half), 1)

        def shifted_rows(lo, count):
            return pltpu.roll(px[pl.ds(lo, count), :], hw, 1)

        def pack(rb):
            lo = pl.multiple_of(rb * half + PAD, PAD)
            first = shifted_rows(lo, hw)
            second = shifted_rows(lo + hw, hw)
            m0, m1 = first[:, :half], second[:, :half]
            pk[1, rb, 0:hw, :] = jnp.where(low_half, m0, pltpu.roll(m1, hw, 1))
            pk[0, rb, 0:hw, :] = jnp.where(low_half, pltpu.roll(m0, hw, 1), m1)
            to_left = jnp.zeros((PAD, half), jnp.float32)
            to_right = to_left
            for k in range(half // PAD):
                part = first if k * PAD < hw else second
                q = k * PAD % hw
                e = part[q:q + PAD, half:]
                here = lane8 == k
                to_left = jnp.where(here, pltpu.roll(e, k, 1) if k else e, to_left)
                to_right = jnp.where(here, pltpu.roll(e, k + 1, 1), to_right)
            pk[0, rb, hw:hw + PAD, :] = to_left
            pk[1, rb, hw:hw + PAD, :] = to_right
            for side, has, target in z_sides:
                @pl.when(has)
                def _():
                    pk_copy(side, target, rb).start()

        def pack_ends():
            for n, lo in ((0, 0), (1, height - PAD)):
                hk[n] = shifted_rows(lo, PAD)[:, :half]
            for side, has, target in z_sides:
                @pl.when(has)
                def _():
                    hk_copy(side, target).start()

        def unpack(rb):
            for side, has, target in z_sides:
                @pl.when(has)
                def _():
                    pk_arrival(side, target, rb).wait_recv()
            lo = pl.multiple_of(rb * half + PAD, PAD)
            from_left, from_right = pr[0, rb, 0:hw, :], pr[1, rb, 0:hw, :]
            for n in range(2):
                start = lo + n * hw
                rolled = shifted_rows(start, hw)
                m = rolled[:, :half]
                fl = pltpu.roll(from_left, hw, 1) if n else from_left
                fr = from_right if n else pltpu.roll(from_right, hw, 1)
                pe[pl.ds(start, hw), half:2 * half] = jnp.where(low_half, fl, m)
                pe[pl.ds(start, hw), 2 * half:3 * half] = rolled[:, half:]
                pe[pl.ds(start, hw), 3 * half:4 * half] = jnp.where(low_half, m, fr)
            cl, cr = pr[0, rb, hw:hw + PAD, :], pr[1, rb, hw:hw + PAD, :]
            for k in range(half // PAD):
                pe[pl.ds(lo + k * PAD, PAD), 0:half] = pltpu.roll(cl, half - 1 - k, 1)
                pe[pl.ds(lo + k * PAD, PAD), 4 * half:5 * half] = pltpu.roll(cr, half - k, 1) if k else cr

        def unpack_ends():
            for side, has, target in z_sides:
                @pl.when(has)
                def _():
                    hk_arrival(side, target).wait_recv()
            low8 = lane8 < hw
            for n, lo in ((0, 0), (1, height - PAD)):
                rolled = shifted_rows(lo, PAD)
                m = rolled[:, :half]
                pe[lo:lo + PAD, half:2 * half] = jnp.where(low8, hr[0, n], m)
                pe[lo:lo + PAD, 2 * half:3 * half] = rolled[:, half:]
                pe[lo:lo + PAD, 3 * half:4 * half] = jnp.where(low8, m, hr[1, n])

        wide = (strips + 2) * half
        step = 2 * PAD

        def weigh(rb):
            @pl.loop(0, half // step, unroll=4)
            def _(c):
                q = pl.multiple_of(c * step, step)
                lo = pl.multiple_of(rb * half + PAD + q, PAD)
                block = pe[pl.ds(lo - PAD, step + 2 * PAD), half:wide - half]
                line = pe[pl.ds(lo, step), :]
                mid = block[PAD:PAD + step]
                east = block[PAD + 1:PAD + 1 + step]
                west = block[PAD - 1:PAD - 1 + step]
                north = pltpu.roll(line, wide - 1, 1)[:, half:wide - half]
                south = pltpu.roll(line, 1, 1)[:, half:wide - half]
                se, sw, sn, ss = mid + east, mid + west, mid + north, mid + south
                across, along = sn * ss, se * sw
                ne, nw = east * sw * across, west * se * across
                nn, ns = north * ss * along, south * sn * along
                scale = relaxation / jnp.maximum((ne + nw) + (nn + ns), 1e-30)
                for n, face in enumerate((ne, nw, nn, ns)):
                    w[n, rb, pl.ds(q, step), :] = face * scale

        peers = sum(jnp.where(has, 1, 0) for _, has, _t in z_sides + x_sides)
        pl.semaphore_wait(barrier, peers)

        for side, has, target in x_sides:
            @pl.when(has)
            def _():
                row_copy(side, target).start()
        own.wait()

        @pl.loop(1, nx)
        def _(rb):
            pack(rb)

        for side, has, target in x_sides:
            @pl.when(has)
            def _():
                row_arrival(side, target).wait_recv()

        @pl.loop(0, 2)
        def _(n):
            pack(n * nx)

        pack_ends()

        @pl.loop(1, 4)
        def _(rb):
            unpack(rb)

        weigh(need_1[0][0])

        def finish(it, k, i, ready):
            rb = pick(k, ready)

            @pl.when(rb >= 0)
            def _():
                partial(it, rb)
                z_send(it, rb)

            @pl.when(k >= nx - 2)
            def _():
                partial(it, jnp.where(i == 0, 0, nx))

            @pl.when(k == nx - 2)
            def _():
                x_send(it, 0)

            @pl.when(k == nx - 1)
            def _():
                x_send(it, 1)

        next_pe = [4 + k for k in range(nx - 4)] + [0, nx, -1, -1]

        @pl.loop(0, nx)
        def _(k):
            i = pick(k, rows_1)
            a_copy(i).wait()
            nxt = pick(k, next_pe)

            @pl.when(nxt >= 0)
            def _():
                unpack(nxt)

            @pl.when(k == nx - 2)
            def _():
                unpack_ends()

            weigh(pick(k, [n[-1] for n in need_1]))
            smooth_row(i, True)
            finish(0, k, i, ready_1)

        x_add(0, 0)
        z_send(0, 0)
        x_add(0, 1)
        z_send(0, last)

        invert(0, need_2[0][0])

        @pl.loop(0, nx)
        def _(k):
            i = pick(k, rows_2)
            invert(0, pick(k, [n[-1] for n in need_2]))
            normalise(i, b, None)
            smooth_row(i, False)
            finish(1, k, i, ready_2)

        x_add(1, 0)
        z_send(1, 0)
        x_add(1, 1)
        z_send(1, last)

        invert(1, need_2[0][-1])

        @pl.loop(0, nx)
        def _(k):
            i = pick(k, rows_2)
            invert(1, pick(k, [need_2[0][0]] + [n[-1] for n in need_2[1:]]))
            normalise(i, d, a)
            o_copy(i).start()

        @pl.loop(0, nx)
        def _(i):
            o_copy(i).wait()

        for side, has, target in z_sides:
            @pl.when(has)
            def _():
                @pl.loop(0, nx + 1)
                def _(rb):
                    for it in range(ITERS):
                        z_copy(it, side, target, rb).wait_send()
                    pk_copy(side, target, rb).wait_send()
                hk_copy(side, target).wait_send()

        for side, has, target in x_sides:
            @pl.when(has)
            def _():
                row_copy(side, target).wait_send()

    return kernel


def local(permeability, basis, support):
    nx, ny, full, _ = basis.shape
    half = full // 2
    size_x, size_y = lax.axis_size("gx"), lax.axis_size("gy")
    height = permeability.shape[0] + half + 2 * PAD
    f32 = jnp.float32
    strips = ny + 1
    scratch = [
        pltpu.VMEM((nx, ny, full + 2 * PAD, full), f32),
        pltpu.VMEM((nx + 2, ny, full + 2 * PAD, full), f32),
        pltpu.VMEM((nx + 2, ny, full + 2 * PAD, full), f32),
        pltpu.VMEM((4, nx + 1, half, strips * half), f32),
        pltpu.VMEM((ITERS, nx + 1, strips, half, half), f32),
        pltpu.VMEM((nx + 1, half, strips * half), f32),
        pltpu.VMEM((ITERS, 2, nx + 1, half, half), f32),
        pltpu.VMEM((ITERS, 2, strips, half, half), f32),
        pltpu.VMEM((height, full), f32),
        pltpu.VMEM((height, (strips + 2) * half), f32),
        pltpu.VMEM((2, nx + 1, half // 2 + PAD, half), f32),
        pltpu.VMEM((2, nx + 1, half // 2 + PAD, half), f32),
        pltpu.VMEM((2, PAD, half), f32),
        pltpu.VMEM((2, 2, PAD, half), f32),
        pltpu.SemaphoreType.DMA((nx,)),
        pltpu.SemaphoreType.DMA,
        pltpu.SemaphoreType.DMA((nx,)),
        pltpu.SemaphoreType.DMA((ITERS, 2, nx + 1)),
        pltpu.SemaphoreType.DMA((ITERS, 2, nx + 1)),
        pltpu.SemaphoreType.DMA((ITERS, 2)),
        pltpu.SemaphoreType.DMA((ITERS, 2)),
        pltpu.SemaphoreType.DMA((2, nx + 1)),
        pltpu.SemaphoreType.DMA((2, nx + 1)),
        pltpu.SemaphoreType.DMA((2,)),
        pltpu.SemaphoreType.DMA((2,)),
        pltpu.SemaphoreType.DMA((2,)),
        pltpu.SemaphoreType.DMA((2,)),
    ]
    return pl.pallas_call(
        make_kernel(nx, ny, size_x, size_y, half),
        out_shape=jax.ShapeDtypeStruct(basis.shape, f32),
        in_specs=[pl.BlockSpec(memory_space=pltpu.HBM)] * 2,
        out_specs=pl.BlockSpec(memory_space=pl.ANY),
        scratch_shapes=scratch,
        compiler_params=pltpu.CompilerParams(
            collective_id=0, has_side_effects=True, vmem_limit_bytes=48 * 1024 * 1024),
        name="smoothing",
    )(permeability, basis)


def solution(mesh):
    placed = (P("gx", "gy"), P("gx", "gy", None, None), P("gx", "gy", None, None))
    return jax.shard_map(
        local, mesh=mesh, in_specs=placed, out_specs=P("gx", "gy", None, None), check_vma=False
    )
```

```python
import jax
import jax.numpy as jnp
from jax import lax
from jax.experimental import pallas as pl
from jax.experimental.pallas import tpu as pltpu
from jax.sharding import PartitionSpec as P

ITERS = 2
MESH = pl.DeviceIdType.MESH
relaxation = 2.0 / 3.0
PAD = 8
CH = 32


def pick(k, table):
    value = jnp.int32(table[-1])
    for n in range(len(table) - 2, -1, -1):
        value = jnp.where(k == n, table[n], value)
    return value


def completed(rows, count):
    done, out = set(), []
    for i in rows:
        done.add(i)
        new = [rb for rb in (i, i + 1) if 0 < rb < count and rb - 1 in done and rb in done]
        assert len(new) <= 1
        out.append(new[0] if new else -1)
    return out


def needed(rows):
    seen, out = set(), []
    for i in rows:
        new = [rb for rb in (i, i + 1) if rb not in seen]
        seen.update(new)
        out.append(new)
    return out


def make_kernel(nx, ny, size_x, size_y, half):
    full = 2 * half
    last = nx
    strips = ny + 1

    def kernel(*refs):
        (perm_h, basis_h, out_h,
         a, b, d, w, s, inv, rz, rx, px, pe, pk, pr, hk, hr,
         a_sem, p_sem, o_sem, zs_sem, zr_sem, xs_sem, xr_sem,
         ps_sem, pr_sem, hs_sem, hr_sem, rs_sem, rr_sem) = refs
        gx, gy = lax.axis_index("gx"), lax.axis_index("gy")
        has_up, has_down = gx > 0, gx < size_x - 1
        has_left, has_right = gy > 0, gy < size_y - 1
        up, down = (gx - 1, gy), (gx + 1, gy)
        left, right = (gx, gy - 1), (gx, gy + 1)
        z_sides = ((0, has_left, left), (1, has_right, right))
        x_sides = ((0, has_up, up), (1, has_down, down))

        rows_1 = list(range(2, nx - 2)) + [1, nx - 2, 0, nx - 1]
        rows_2 = list(range(3, nx - 3)) + [2, nx - 3, 1, nx - 2, 0, nx - 1]
        need_1, need_2 = needed(rows_1), needed(rows_2)
        ready_1, ready_2 = completed(rows_1, nx), completed(rows_2, nx)
        halo = half // 2 + PAD
        height = px.shape[0]
        length = height - 2 * halo
        hw = half // 2

        def a_copy(i):
            return pltpu.make_async_copy(basis_h.at[i], a.at[i, :, pl.ds(PAD, full), :], a_sem.at[i])

        def row_copy(side, target):
            src = 0 if side == 0 else length - halo
            dst = height - halo if side == 0 else 0
            return pltpu.make_async_remote_copy(
                src_ref=perm_h.at[pl.ds(src, halo), :], dst_ref=px.at[pl.ds(dst, halo), :],
                send_sem=rs_sem.at[side], recv_sem=rr_sem.at[1 - side],
                device_id=target, device_id_type=MESH)

        def row_arrival(side, target):
            dst = 0 if side == 0 else height - halo
            return pltpu.make_async_remote_copy(
                src_ref=perm_h.at[pl.ds(0, halo), :], dst_ref=px.at[pl.ds(dst, halo), :],
                send_sem=rs_sem.at[side], recv_sem=rr_sem.at[side],
                device_id=target, device_id_type=MESH)

        def pk_copy(side, target, rb):
            return pltpu.make_async_remote_copy(
                src_ref=pk.at[side, rb], dst_ref=pr.at[1 - side, rb],
                send_sem=ps_sem.at[side, rb], recv_sem=pr_sem.at[1 - side, rb],
                device_id=target, device_id_type=MESH)

        def pk_arrival(side, target, rb):
            return pltpu.make_async_remote_copy(
                src_ref=pk.at[side, rb], dst_ref=pr.at[side, rb],
                send_sem=ps_sem.at[side, rb], recv_sem=pr_sem.at[side, rb],
                device_id=target, device_id_type=MESH)

        def hk_copy(side, target):
            return pltpu.make_async_remote_copy(
                src_ref=hk, dst_ref=hr.at[1 - side],
                send_sem=hs_sem.at[side], recv_sem=hr_sem.at[1 - side],
                device_id=target, device_id_type=MESH)

        def hk_arrival(side, target):
            return pltpu.make_async_remote_copy(
                src_ref=hk, dst_ref=hr.at[side],
                send_sem=hs_sem.at[side], recv_sem=hr_sem.at[side],
                device_id=target, device_id_type=MESH)

        def o_copy(i):
            return pltpu.make_async_copy(a.at[i, :, pl.ds(PAD, full), :], out_h.at[i], o_sem.at[i])

        def z_copy(it, side, target, rb):
            strip = 0 if side == 0 else strips - 1
            return pltpu.make_async_remote_copy(
                src_ref=s.at[it, rb, strip], dst_ref=rz.at[it, 1 - side, rb],
                send_sem=zs_sem.at[it, side, rb], recv_sem=zr_sem.at[it, 1 - side, rb],
                device_id=target, device_id_type=MESH)

        def z_arrival(it, side, target, rb):
            return pltpu.make_async_remote_copy(
                src_ref=s.at[it, rb, 0], dst_ref=rz.at[it, side, rb],
                send_sem=zs_sem.at[it, side, rb], recv_sem=zr_sem.at[it, side, rb],
                device_id=target, device_id_type=MESH)

        def x_copy(it, side, target):
            rb = 0 if side == 0 else last
            return pltpu.make_async_remote_copy(
                src_ref=s.at[it, rb], dst_ref=rx.at[it, 1 - side],
                send_sem=xs_sem.at[it, side], recv_sem=xr_sem.at[it, 1 - side],
                device_id=target, device_id_type=MESH)

        def x_arrival(it, side, target):
            return pltpu.make_async_remote_copy(
                src_ref=s.at[it, 0], dst_ref=rx.at[it, side],
                send_sem=xs_sem.at[it, side], recv_sem=xr_sem.at[it, side],
                device_id=target, device_id_type=MESH)

        barrier = pltpu.get_barrier_semaphore()
        for _, has, target in z_sides + x_sides:
            @pl.when(has)
            def _():
                pl.semaphore_signal(barrier, inc=1, device_id=target, device_id_type=MESH)

        own = pltpu.make_async_copy(perm_h, px.at[pl.ds(halo, length), :], p_sem)
        own.start()

        @pl.loop(0, nx)
        def _(k):
            a_copy(pick(k, rows_1)).start()

        edge = jnp.zeros((PAD, full), jnp.float32)
        blank = jnp.zeros((half, half), jnp.float32)

        @pl.loop(0, nx)
        def _(i):
            for j in range(ny):
                a[i, j, 0:PAD, :] = edge
                a[i, j, PAD + full:, :] = edge
                b[i + 1, j, 0:PAD, :] = edge
                b[i + 1, j, PAD + full:, :] = edge

        for buf in (b, d):
            for j in range(ny):
                for r in range(0, full, half):
                    buf[0, j, PAD + r:PAD + r + half, :] = jnp.zeros((half, full), jnp.float32)
                    buf[nx + 1, j, PAD + r:PAD + r + half, :] = jnp.zeros((half, full), jnp.float32)

        for side, has, _t in z_sides:
            @pl.when(jnp.logical_not(has))
            def _():
                @pl.loop(0, nx + 1)
                def _(rb):
                    for it in range(ITERS):
                        rz[it, side, rb] = blank
                    pr[side, rb] = jnp.zeros((hw + PAD, half), jnp.float32)
                hr[side] = jnp.zeros((2, PAD, half), jnp.float32)

        for side, has, _t in x_sides:
            @pl.when(jnp.logical_not(has))
            def _():
                lo = 0 if side == 0 else height - halo
                px[lo:lo + halo, :] = jnp.zeros((halo, full), jnp.float32)

        lanes = lax.broadcasted_iota(jnp.int32, (CH, full), 1)
        not_last, not_first = lanes < full - 1, lanes > 0

        def smooth_row(i, first):
            for j in range(ny):
                for r in range(0, full, CH):
                    lo = PAD + r
                    rb = i + r // half
                    q = r % half

                    def load(shift):
                        if first:
                            return a[i, j, lo + shift:lo + shift + CH, :]
                        return b[i + 1, j, lo + shift:lo + shift + CH, :]

                    def weight(n):
                        return w[n, rb, q:q + CH, j * half:j * half + full]

                    x = load(0)
                    ahead = jnp.where(not_last, pltpu.roll(x, full - 1, 1), 0.0)
                    behind = jnp.where(not_first, pltpu.roll(x, 1, 1), 0.0)
                    new = (1.0 - relaxation) * x + weight(0) * load(1) + weight(1) * load(-1)
                    new = new + weight(2) * ahead + weight(3) * behind
                    mask = x if first else a[i, j, lo:lo + CH, :]
                    new = jnp.where(mask > 0, new, 0.0)
                    if first:
                        b[i + 1, j, lo:lo + CH, :] = new
                    else:
                        d[i + 1, j, lo:lo + CH, :] = new

        def partial(it, rb):
            src = b if it == 0 else d
            for c in range(strips):
                for r in range(0, half, CH):
                    total = None
                    for j, lane in ((c - 1, half), (c, 0)):
                        if 0 <= j < ny:
                            low = src[rb, j, PAD + half + r:PAD + half + r + CH, lane:lane + half]
                            high = src[rb + 1, j, PAD + r:PAD + r + CH, lane:lane + half]
                            term = low + high
                            total = term if total is None else total + term
                    s[it, rb, c, r:r + CH, :] = total

        def z_send(it, rb):
            for side, has, target in z_sides:
                @pl.when(has)
                def _():
                    z_copy(it, side, target, rb).start()

        def invert(it, rb):
            for side, has, target in z_sides:
                @pl.when(has)
                def _():
                    z_arrival(it, side, target, rb).wait_recv()
            for c in range(strips):
                for r in range(0, half, CH):
                    total = s[it, rb, c, r:r + CH, :]
                    if c == 0:
                        total = total + rz[it, 0, rb, r:r + CH, :]
                    if c == strips - 1:
                        total = total + rz[it, 1, rb, r:r + CH, :]
                    inv[rb, r:r + CH, c * half:(c + 1) * half] = 1.0 / jnp.where(total > 0, total, 1.0)

        def x_send(it, side):
            _, has, target = x_sides[side]

            @pl.when(has)
            def _():
                x_copy(it, side, target).start()

        def x_add(it, side):
            _, has, target = x_sides[side]
            rb = 0 if side == 0 else last

            @pl.when(has)
            def _():
                x_copy(it, side, target).wait_send()
                x_arrival(it, side, target).wait_recv()
                for c in range(strips):
                    s[it, rb, c] = s[it, rb, c] + rx[it, side, c]

        def normalise(i, src, dst):
            for j in range(ny):
                for r in range(0, full, CH):
                    rb = i + r // half
                    q = r % half
                    lo = PAD + r
                    value = src[i + 1, j, lo:lo + CH, :] * inv[rb, q:q + CH, j * half:j * half + full]
                    if dst is None:
                        src[i + 1, j, lo:lo + CH, :] = value
                    else:
                        dst[i, j, lo:lo + CH, :] = value

        lane = lax.broadcasted_iota(jnp.int32, (hw, half), 1)
        low_half = lane < hw
        lane8 = lax.broadcasted_iota(jnp.int32, (PAD, half), 1)

        def shifted_rows(lo, count):
            return pltpu.roll(px[pl.ds(lo, count), :], hw, 1)

        def pack(rb):
            lo = pl.multiple_of(rb * half + PAD, PAD)
            first = shifted_rows(lo, hw)
            second = shifted_rows(lo + hw, hw)
            m0, m1 = first[:, :half], second[:, :half]
            pk[1, rb, 0:hw, :] = jnp.where(low_half, m0, pltpu.roll(m1, hw, 1))
            pk[0, rb, 0:hw, :] = jnp.where(low_half, pltpu.roll(m0, hw, 1), m1)
            to_left = jnp.zeros((PAD, half), jnp.float32)
            to_right = to_left
            for k in range(half // PAD):
                part = first if k * PAD < hw else second
                q = k * PAD % hw
                e = part[q:q + PAD, half:]
                here = lane8 == k
                to_left = jnp.where(here, pltpu.roll(e, k, 1) if k else e, to_left)
                to_right = jnp.where(here, pltpu.roll(e, k + 1, 1), to_right)
            pk[0, rb, hw:hw + PAD, :] = to_left
            pk[1, rb, hw:hw + PAD, :] = to_right
            for side, has, target in z_sides:
                @pl.when(has)
                def _():
                    pk_copy(side, target, rb).start()

        def pack_ends():
            for n, lo in ((0, 0), (1, height - PAD)):
                hk[n] = shifted_rows(lo, PAD)[:, :half]
            for side, has, target in z_sides:
                @pl.when(has)
                def _():
                    hk_copy(side, target).start()

        def unpack(rb):
            for side, has, target in z_sides:
                @pl.when(has)
                def _():
                    pk_arrival(side, target, rb).wait_recv()
            lo = pl.multiple_of(rb * half + PAD, PAD)
            from_left, from_right = pr[0, rb, 0:hw, :], pr[1, rb, 0:hw, :]
            for n in range(2):
                start = lo + n * hw
                rolled = shifted_rows(start, hw)
                m = rolled[:, :half]
                fl = pltpu.roll(from_left, hw, 1) if n else from_left
                fr = from_right if n else pltpu.roll(from_right, hw, 1)
                pe[pl.ds(start, hw), half:2 * half] = jnp.where(low_half, fl, m)
                pe[pl.ds(start, hw), 2 * half:3 * half] = rolled[:, half:]
                pe[pl.ds(start, hw), 3 * half:4 * half] = jnp.where(low_half, m, fr)
            cl, cr = pr[0, rb, hw:hw + PAD, :], pr[1, rb, hw:hw + PAD, :]
            for k in range(half // PAD):
                pe[pl.ds(lo + k * PAD, PAD), 0:half] = pltpu.roll(cl, half - 1 - k, 1)
                pe[pl.ds(lo + k * PAD, PAD), 4 * half:5 * half] = pltpu.roll(cr, half - k, 1) if k else cr

        def unpack_ends():
            for side, has, target in z_sides:
                @pl.when(has)
                def _():
                    hk_arrival(side, target).wait_recv()
            low8 = lane8 < hw
            for n, lo in ((0, 0), (1, height - PAD)):
                rolled = shifted_rows(lo, PAD)
                m = rolled[:, :half]
                pe[lo:lo + PAD, half:2 * half] = jnp.where(low8, hr[0, n], m)
                pe[lo:lo + PAD, 2 * half:3 * half] = rolled[:, half:]
                pe[lo:lo + PAD, 3 * half:4 * half] = jnp.where(low8, m, hr[1, n])

        wide = (strips + 2) * half
        step = 2 * PAD

        def weigh(rb):
            @pl.loop(0, half // step, unroll=8)
            def _(c):
                q = pl.multiple_of(c * step, step)
                lo = pl.multiple_of(rb * half + PAD + q, PAD)
                block = pe[pl.ds(lo - PAD, step + 2 * PAD), half:wide - half]
                line = pe[pl.ds(lo, step), :]
                mid = block[PAD:PAD + step]
                east = block[PAD + 1:PAD + 1 + step]
                west = block[PAD - 1:PAD - 1 + step]
                north = pltpu.roll(line, wide - 1, 1)[:, half:wide - half]
                south = pltpu.roll(line, 1, 1)[:, half:wide - half]
                se, sw, sn, ss = mid + east, mid + west, mid + north, mid + south
                across, along = sn * ss, se * sw
                ne, nw = east * sw * across, west * se * across
                nn, ns = north * ss * along, south * sn * along
                scale = relaxation / jnp.maximum((ne + nw) + (nn + ns), 1e-30)
                for n, face in enumerate((ne, nw, nn, ns)):
                    w[n, rb, pl.ds(q, step), :] = face * scale

        peers = sum(jnp.where(has, 1, 0) for _, has, _t in z_sides + x_sides)
        pl.semaphore_wait(barrier, peers)

        for side, has, target in x_sides:
            @pl.when(has)
            def _():
                row_copy(side, target).start()
        own.wait()

        @pl.loop(1, nx)
        def _(rb):
            pack(rb)

        for side, has, target in x_sides:
            @pl.when(has)
            def _():
                row_arrival(side, target).wait_recv()

        @pl.loop(0, 2)
        def _(n):
            pack(n * nx)

        pack_ends()

        @pl.loop(1, 4)
        def _(rb):
            unpack(rb)

        weigh(need_1[0][0])

        def finish(it, k, i, ready):
            rb = pick(k, ready)

            @pl.when(rb >= 0)
            def _():
                partial(it, rb)
                z_send(it, rb)

            @pl.when(k >= nx - 2)
            def _():
                partial(it, jnp.where(i == 0, 0, nx))

            @pl.when(k == nx - 2)
            def _():
                x_send(it, 0)

            @pl.when(k == nx - 1)
            def _():
                x_send(it, 1)

        next_pe = [4 + k for k in range(nx - 4)] + [0, nx, -1, -1]

        @pl.loop(0, nx)
        def _(k):
            i = pick(k, rows_1)
            a_copy(i).wait()
            nxt = pick(k, next_pe)

            @pl.when(nxt >= 0)
            def _():
                unpack(nxt)

            @pl.when(k == nx - 2)
            def _():
                unpack_ends()

            weigh(pick(k, [n[-1] for n in need_1]))
            smooth_row(i, True)
            finish(0, k, i, ready_1)

        x_add(0, 0)
        z_send(0, 0)
        x_add(0, 1)
        z_send(0, last)

        invert(0, need_2[0][0])

        @pl.loop(0, nx)
        def _(k):
            i = pick(k, rows_2)
            invert(0, pick(k, [n[-1] for n in need_2]))
            normalise(i, b, None)
            smooth_row(i, False)
            finish(1, k, i, ready_2)

        x_add(1, 0)
        z_send(1, 0)
        x_add(1, 1)
        z_send(1, last)

        invert(1, need_2[0][-1])

        @pl.loop(0, nx)
        def _(k):
            i = pick(k, rows_2)
            invert(1, pick(k, [need_2[0][0]] + [n[-1] for n in need_2[1:]]))
            normalise(i, d, a)
            o_copy(i).start()

        @pl.loop(0, nx)
        def _(i):
            o_copy(i).wait()

        for side, has, target in z_sides:
            @pl.when(has)
            def _():
                @pl.loop(0, nx + 1)
                def _(rb):
                    for it in range(ITERS):
                        z_copy(it, side, target, rb).wait_send()
                    pk_copy(side, target, rb).wait_send()
                hk_copy(side, target).wait_send()

        for side, has, target in x_sides:
            @pl.when(has)
            def _():
                row_copy(side, target).wait_send()

    return kernel


def local(permeability, basis, support):
    nx, ny, full, _ = basis.shape
    half = full // 2
    size_x, size_y = lax.axis_size("gx"), lax.axis_size("gy")
    height = permeability.shape[0] + half + 2 * PAD
    f32 = jnp.float32
    strips = ny + 1
    scratch = [
        pltpu.VMEM((nx, ny, full + 2 * PAD, full), f32),
        pltpu.VMEM((nx + 2, ny, full + 2 * PAD, full), f32),
        pltpu.VMEM((nx + 2, ny, full + 2 * PAD, full), f32),
        pltpu.VMEM((4, nx + 1, half, strips * half), f32),
        pltpu.VMEM((ITERS, nx + 1, strips, half, half), f32),
        pltpu.VMEM((nx + 1, half, strips * half), f32),
        pltpu.VMEM((ITERS, 2, nx + 1, half, half), f32),
        pltpu.VMEM((ITERS, 2, strips, half, half), f32),
        pltpu.VMEM((height, full), f32),
        pltpu.VMEM((height, (strips + 2) * half), f32),
        pltpu.VMEM((2, nx + 1, half // 2 + PAD, half), f32),
        pltpu.VMEM((2, nx + 1, half // 2 + PAD, half), f32),
        pltpu.VMEM((2, PAD, half), f32),
        pltpu.VMEM((2, 2, PAD, half), f32),
        pltpu.SemaphoreType.DMA((nx,)),
        pltpu.SemaphoreType.DMA,
        pltpu.SemaphoreType.DMA((nx,)),
        pltpu.SemaphoreType.DMA((ITERS, 2, nx + 1)),
        pltpu.SemaphoreType.DMA((ITERS, 2, nx + 1)),
        pltpu.SemaphoreType.DMA((ITERS, 2)),
        pltpu.SemaphoreType.DMA((ITERS, 2)),
        pltpu.SemaphoreType.DMA((2, nx + 1)),
        pltpu.SemaphoreType.DMA((2, nx + 1)),
        pltpu.SemaphoreType.DMA((2,)),
        pltpu.SemaphoreType.DMA((2,)),
        pltpu.SemaphoreType.DMA((2,)),
        pltpu.SemaphoreType.DMA((2,)),
    ]
    return pl.pallas_call(
        make_kernel(nx, ny, size_x, size_y, half),
        out_shape=jax.ShapeDtypeStruct(basis.shape, f32),
        in_specs=[pl.BlockSpec(memory_space=pltpu.HBM)] * 2,
        out_specs=pl.BlockSpec(memory_space=pl.ANY),
        scratch_shapes=scratch,
        compiler_params=pltpu.CompilerParams(
            collective_id=0, has_side_effects=True, vmem_limit_bytes=48 * 1024 * 1024),
        name="smoothing",
    )(*[pltpu.with_memory_space_constraint(x, pltpu.HBM) for x in (permeability, basis)])


def solution(mesh):
    placed = (P("gx", "gy"), P("gx", "gy", None, None), P("gx", "gy", None, None))
    return jax.shard_map(
        local, mesh=mesh, in_specs=placed, out_specs=P("gx", "gy", None, None), check_vma=False
    )
```
